32 devices in a mesh: seq: 16 (over z, y, core), head: 2 (over x).
Axes of the slice: x: 2, y: 2, z: 4, core: 2. Of those that a mesh axis runs over, the one named last changes fastest.
Arguments:
- latent_queries: bfloat16 [2048, 128, 576], P('seq', 'head'), may hold values from -16 to 16
- latent_keys: bfloat16 [1024, 576], P('seq'), may hold values from -6 to 6
- index_queries: bfloat16 [2048, 64, 128], P('seq', 'head'), may hold values from -8 to 8
- index_keys: bfloat16 [1024, 128], P('seq'), may hold values from -6 to 6
- head_weights: float32 [2048, 64], P('seq', 'head'), may hold values from -18 to 18
- visible: int32 [2048], P('seq'), may hold values from 1 to 1024, as said below
Outputs:
- grad_index_queries: bfloat16 [2048, 64, 128], P('seq', 'head')
- grad_head_weights: float32 [2048, 64], P('seq', 'head')
- grad_index_keys: float32 [1024, 128], P('seq')
The draws below stay inside these ranges and needn't reach their ends.
Inputs may be any that keep to these rules, and one draw needn't show every extreme that they name: Row t sees keys 0 to visible[t] - 1, never more than (t * 1024) // 2048 + 1 of them; the last row sees all 1024 keys.
All inputs are finite; a program needn't handle non-finite values.
Results may differ from the reference program's by a relative error of at most 0.0049.
Values may be sent and summed in bfloat16 or wider, within the bound.
A program may use at most 128 MiB of HBM per device.

```python
import math
import jax
import jax.numpy as jnp
from jax import lax

LATENT = 576
MLA_HEADS = 128
INDEX_HEADS = 64
INDEX_DIM = 128
QUERIES = 2048
KEYS = 1024


def visible_counts(key):
    positions = jnp.arange(QUERIES, dtype=jnp.int32)
    baseline = positions * KEYS // QUERIES + 1
    jitter = jax.random.randint(jax.random.fold_in(key, 11), (QUERIES,), 0, KEYS // 8 + 1)
    jitter = jnp.where(positions == QUERIES - 1, 0, jitter)
    lowest = jnp.minimum(baseline, 2)
    return jnp.maximum(baseline - jitter, lowest).astype(jnp.int32)


def make_keys(key, salt, width):
    subkey = jax.random.fold_in(key, salt)
    return jnp.clip(jax.random.normal(subkey, (KEYS, width), jnp.float32), -6.0, 6.0)


def draw_visible(key, part):
    return visible_counts(key)


def draw_latent_keys(key, part):
    return make_keys(key, 1, LATENT).astype(jnp.bfloat16)


def draw_index_keys(key, part):
    return make_keys(key, 2, INDEX_DIM).astype(jnp.bfloat16)


def draw_latent_queries(key, part):
    full_shape = (QUERIES, MLA_HEADS, LATENT)
    subkey = jax.random.fold_in(key, 3)
    values = jnp.clip(jax.random.normal(subkey, full_shape, jnp.float32), -6.0, 6.0) * 2.3
    return values.astype(jnp.bfloat16)


def draw_index_queries(key, part):
    full_shape = (QUERIES, INDEX_HEADS, INDEX_DIM)
    subkey = jax.random.fold_in(key, 5)
    values = jnp.clip(jax.random.normal(subkey, full_shape, jnp.float32), -6.0, 6.0)
    return values.astype(jnp.bfloat16)


def draw_head_weights(key, part):
    subkey = jax.random.fold_in(key, 6)
    values = jnp.clip(jax.random.normal(subkey, (QUERIES, INDEX_HEADS), jnp.float32), -6.0, 6.0) * 3.0
    return values.astype(jnp.float32)


def setup_inputs(seed: int = 0) -> dict:
    streams_of = jax.random.split(jax.random.key(seed), 7)
    return {
        "latent_queries": draw_latent_queries(jax.random.fold_in(streams_of[6], 71), 0),
        "latent_keys": draw_latent_keys(jax.random.fold_in(streams_of[6], 71), 0),
        "index_queries": draw_index_queries(jax.random.fold_in(streams_of[6], 71), 0),
        "index_keys": draw_index_keys(jax.random.fold_in(streams_of[6], 71), 0),
        "head_weights": draw_head_weights(jax.random.fold_in(streams_of[6], 71), 0),
        "visible": draw_visible(jax.random.fold_in(streams_of[6], 71), 0),
    }


mla_scale = 192.0 ** -0.5
loss_weight = 16.0
neg_fill = -1.0e30


def reference(latent_queries, latent_keys, index_queries, index_keys, head_weights, visible):
    query_count = latent_queries.shape[0]
    key_count = latent_keys.shape[0]
    row_block = math.gcd(query_count, 128)
    block_count = query_count // row_block
    latent_wide = latent_keys.astype(jnp.float32)
    index_wide = index_keys.astype(jnp.float32)
    dot_scale = INDEX_DIM ** -0.5
    head_scale = INDEX_HEADS ** -0.5
    columns = jnp.arange(key_count, dtype=jnp.int32)

    def one_block(key_grad, inputs):
        lat_rows, idx_rows, weight_rows, seen_rows = inputs
        seen = columns[None, :] < seen_rows[:, None]
        scores = jnp.einsum("thl,kl->thk", lat_rows.astype(jnp.float32), latent_wide, precision=lax.Precision.HIGHEST) * mla_scale
        scores = jnp.where(seen[:, None, :], scores, neg_fill)
        maxima = jnp.max(scores, axis=2, keepdims=True)
        mla_norm = maxima + jnp.log(jnp.sum(jnp.exp(scores - maxima), axis=2, keepdims=True))
        target = jnp.sum(jnp.exp(scores - mla_norm), axis=1) / MLA_HEADS
        products = jnp.einsum("thd,kd->thk", idx_rows.astype(jnp.float32), index_wide, precision=lax.Precision.HIGHEST) * dot_scale
        active = jnp.maximum(products, 0.0)
        logits = jnp.sum(weight_rows[:, :, None] * active, axis=1) * head_scale
        logits = jnp.where(seen, logits, neg_fill)
        row_peak = jnp.max(logits, axis=1, keepdims=True)
        weights = jnp.exp(logits - row_peak)
        index_prob = weights / jnp.sum(weights, axis=1, keepdims=True)
        slope = loss_weight * (index_prob - target)
        edge_grad = jnp.where(products > 0.0, slope[:, None, :] * (weight_rows * head_scale)[:, :, None], 0.0).astype(jnp.bfloat16)
        edge_wide = edge_grad.astype(jnp.float32)
        query_grad = (jnp.einsum("thk,kd->thd", edge_wide, index_wide, precision=lax.Precision.HIGHEST) * dot_scale).astype(jnp.bfloat16)
        weight_grad = jnp.sum(slope[:, None, :] * active, axis=2) * head_scale
        key_term = jnp.einsum("thk,thd->kd", edge_wide, idx_rows.astype(jnp.float32), precision=lax.Precision.HIGHEST) * dot_scale
        return key_grad + key_term, (query_grad, weight_grad)

    inputs = (
        latent_queries.reshape(block_count, row_block, MLA_HEADS, LATENT),
        index_queries.reshape(block_count, row_block, INDEX_HEADS, INDEX_DIM),
        head_weights.reshape(block_count, row_block, INDEX_HEADS),
        visible.reshape(block_count, row_block),
    )
    key_grad, stacked = lax.scan(one_block, jnp.zeros((key_count, INDEX_DIM), jnp.float32), inputs)
    grad_index_queries = stacked[0].reshape(query_count, INDEX_HEADS, INDEX_DIM)
    grad_head_weights = stacked[1].reshape(query_count, INDEX_HEADS)
    return (grad_index_queries, grad_head_weights, key_grad)
```

```python
import functools
import jax
import jax.numpy as jnp
from jax import lax
from jax.experimental import pallas as pl
from jax.experimental.pallas import tpu as pltpu
from jax.sharding import PartitionSpec as P

MLA_HEADS = 128
INDEX_HEADS = 64
LOG2E = 1.4426950408889634

mla_scale = 192.0 ** (-0.5)
loss_weight = 16.0
neg_fill = -1e30
MESH = pl.DeviceIdType.MESH
VMEM = pltpu.VMEM


def line_sizes(n):
    ny = 2 if n <= 16 else 4
    return n // (2 * ny), ny


def remote(src, dst, ssem, rsem, device):
    return pltpu.make_async_remote_copy(
        src_ref=src, dst_ref=dst, send_sem=ssem, recv_sem=rsem, device_id=device, device_id_type=MESH
    )


def gather_kernel(n, lat_ref, idx_ref, lat_all, idx_all, lsem, zs, zr, ys, yr, cs, cr):
    nz, ny = line_sizes(n)
    me = lax.axis_index("seq")
    core = me % 2
    y = (me // 2) % ny
    z = me // (2 * ny)
    size = lat_ref.shape[0]

    def at(zz, yy, cc):
        return (zz * ny + yy) * 2 + cc

    zpeers = [(z + k) % nz for k in range(1, nz)]
    ypeers = [(y + k) % ny for k in range(1, ny)]
    barrier = pltpu.get_barrier_semaphore()
    for zz in zpeers:
        pl.semaphore_signal(barrier, inc=1, device_id={"seq": at(zz, y, core)}, device_id_type=MESH)
    for yy in ypeers:
        pl.semaphore_signal(barrier, inc=1, device_id={"seq": at(z, yy, core)}, device_id_type=MESH)
    pl.semaphore_signal(barrier, inc=1, device_id={"seq": at(z, y, 1 - core)}, device_id_type=MESH)

    def rows(ref, owner):
        return ref.at[pl.ds(pl.multiple_of(owner * size, size), size), :]

    locals_ = [
        pltpu.make_async_copy(lat_ref, rows(lat_all, me), lsem.at[0]),
        pltpu.make_async_copy(idx_ref, rows(idx_all, me), lsem.at[1]),
    ]
    for c in locals_:
        c.start()
    pl.semaphore_wait(barrier, nz - 1 + ny - 1 + 1)
    pending = []

    def send(owner, device, ssem, rsem, first):
        src_l = lat_ref if first else rows(lat_all, owner)
        src_i = idx_ref if first else rows(idx_all, owner)
        out = [
            remote(src_l, rows(lat_all, owner), ssem.at[0], rsem.at[0], {"seq": device}),
            remote(src_i, rows(idx_all, owner), ssem.at[1], rsem.at[1], {"seq": device}),
        ]
        for c in out:
            c.start()
        pending.extend(out)

    def receive(owner, sems, rsem):
        remote(lat_ref, rows(lat_all, owner), sems.at[0], rsem.at[0], {"seq": me}).wait_recv()
        remote(idx_ref, rows(idx_all, owner), sems.at[1], rsem.at[1], {"seq": me}).wait_recv()

    for k in range(1, nz):
        send(me, at((z + k) % nz, y, core), zs.at[k], zr.at[k], True)
    for j in range(1, ny):
        send(me, at(z, (y + j) % ny, core), ys.at[0, j], yr.at[0, j], True)
    send(me, at(z, y, 1 - core), cs.at[0, 0], cr.at[0, 0], True)
    for k in range(1, nz):
        owner = at((z - k + nz) % nz, y, core)
        receive(owner, zs.at[k], zr.at[k])
        for j in range(1, ny):
            send(owner, at(z, (y + j) % ny, core), ys.at[k, j], yr.at[k, j], False)
        send(owner, at(z, y, 1 - core), cs.at[k, 0], cr.at[k, 0], False)
    for k in range(nz):
        for j in range(1, ny):
            owner = at((z - k + nz) % nz, (y - j + ny) % ny, core)
            receive(owner, ys.at[k, j], yr.at[k, j])
            send(owner, at(z, y, 1 - core), cs.at[k, j], cr.at[k, j], False)
    for k in range(nz):
        for j in range(ny):
            owner = at((z - k + nz) % nz, (y - j + ny) % ny, 1 - core)
            receive(owner, cs.at[k, j], cr.at[k, j])
    for c in pending:
        c.wait_send()
    for c in locals_:
        c.wait()


def gather_keys(n, latent_keys, index_keys):
    nz, ny = line_sizes(n)
    size, width = latent_keys.shape
    depth = index_keys.shape[1]
    dma = pltpu.SemaphoreType.DMA
    return pl.pallas_call(
        functools.partial(gather_kernel, n),
        out_shape=(
            jax.ShapeDtypeStruct((n * size, width), jnp.bfloat16),
            jax.ShapeDtypeStruct((n * size, depth), jnp.bfloat16),
        ),
        in_specs=[pl.BlockSpec(memory_space=VMEM)] * 2,
        out_specs=(pl.BlockSpec(memory_space=VMEM),) * 2,
        scratch_shapes=[
            dma((2,)),
            dma((nz, 2)), dma((nz, 2)),
            dma((nz, ny, 2)), dma((nz, ny, 2)),
            dma((nz, ny, 2)), dma((nz, ny, 2)),
        ],
        compiler_params=pltpu.CompilerParams(collective_id=0, has_side_effects=True),
        name="gather_keys",
    )(latent_keys, index_keys)


def forward_kernel(sub, vis_ref, lat_ref, idx_ref, w_ref, lk_ref, ik_ref, logit_ref, target_ref):
    row_count, heads, width = lat_ref.shape
    gheads = idx_ref.shape[1]
    key_count = lk_ref.shape[0]
    step = pl.program_id(0)
    ids = lax.broadcasted_iota(jnp.int32, (1, key_count), 1)
    contract = (((1,), (1,)), ((), ()))
    depth_scale = float(idx_ref.shape[2]) ** (-0.5) * INDEX_HEADS ** (-0.5)
    c = mla_scale * LOG2E
    for first in range(0, row_count, sub):
        scores = lax.dot_general(
            lat_ref[first : first + sub].reshape(sub * heads, width), lk_ref[...], contract,
            preferred_element_type=jnp.float32,
        )
        targets = []
        for r in range(sub):
            seen = ids < vis_ref[step * row_count + first + r]
            s = jnp.where(seen, scores[r * heads : (r + 1) * heads], neg_fill)
            peak = jnp.max(s, axis=1, keepdims=True)
            e = jnp.exp2((s - peak) * c)
            scale = (1.0 / MLA_HEADS) / jnp.sum(e, axis=1, keepdims=True)
            targets.append(jnp.sum(e * scale, axis=0, keepdims=True))
        target_ref[first : first + sub, :] = jnp.concatenate(targets, axis=0).astype(target_ref.dtype)
        products = lax.dot_general(
            idx_ref[first : first + sub].reshape(sub * gheads, idx_ref.shape[2]), ik_ref[...], contract,
            preferred_element_type=jnp.float32,
        )
        logits = []
        for r in range(sub):
            p = jnp.maximum(products[r * gheads : (r + 1) * gheads], 0.0)
            w = w_ref[pl.ds((first + r) * gheads, gheads), :] * depth_scale
            logits.append(jnp.sum(p * w, axis=0, keepdims=True))
        logit_ref[first : first + sub, :] = jnp.concatenate(logits, axis=0)


def forward(latent_queries, index_queries, weights, visible, lat_all, idx_all, rows=16, sub=8):
    row_count, heads, width = latent_queries.shape
    gheads, depth = index_queries.shape[1:]
    key_count = lat_all.shape[0]
    grid = (row_count // rows,)
    return pl.pallas_call(
        functools.partial(forward_kernel, sub),
        out_shape=(
            jax.ShapeDtypeStruct((row_count, key_count), jnp.float32),
            jax.ShapeDtypeStruct((row_count, key_count), jnp.float32),
        ),
        grid_spec=pltpu.PrefetchScalarGridSpec(
            num_scalar_prefetch=1,
            grid=grid,
            in_specs=[
                pl.BlockSpec((rows, heads, width), lambda i, v: (i, 0, 0)),
                pl.BlockSpec((rows, gheads, depth), lambda i, v: (i, 0, 0)),
                pl.BlockSpec((rows * gheads, 1), lambda i, v: (i, 0)),
                pl.BlockSpec((key_count, width), lambda i, v: (0, 0)),
                pl.BlockSpec((key_count, depth), lambda i, v: (0, 0)),
            ],
            out_specs=(
                pl.BlockSpec((rows, key_count), lambda i, v: (i, 0)),
                pl.BlockSpec((rows, key_count), lambda i, v: (i, 0)),
            ),
        ),
        name="forward_rows",
    )(visible, latent_queries, index_queries, weights, lat_all, idx_all)


def exchange_kernel(nh, logit_ref, target_ref, vis_ref, slope_ref, logit_got, target_got, target_out, part, got, ss, rs):
    me = lax.axis_index("head")
    share = logit_ref.shape[0] // nh

    def rows_of(owner):
        return pl.ds(pl.multiple_of(owner * share, share), share)

    mine = rows_of(me)
    peers = [(me + k) % nh for k in range(1, nh)]
    sources = [(me - k + nh) % nh for k in range(1, nh)]
    barrier = pltpu.get_barrier_semaphore()
    for peer in peers:
        pl.semaphore_signal(barrier, inc=1, device_id={"head": peer}, device_id_type=MESH)
    target_out[...] = target_ref[...].astype(jnp.bfloat16)
    pl.semaphore_wait(barrier, nh - 1)
    first, second, third = [], [], []
    for k, peer in enumerate(peers):
        first.append(remote(logit_ref.at[rows_of(peer), :], logit_got.at[k], ss.at[0, k], rs.at[0, k], {"head": peer}))
        first[-1].start()
    for k, peer in enumerate(peers):
        second.append(remote(target_out.at[rows_of(peer), :], target_got.at[k], ss.at[1, k], rs.at[1, k], {"head": peer}))
        second[-1].start()
    logits = logit_ref[mine, :]
    for k in range(nh - 1):
        first[k].wait_recv()
        logits = logits + logit_got[k]
    ids = lax.broadcasted_iota(jnp.int32, logits.shape, 1)
    logits = jnp.where(ids < vis_ref[mine, :], logits, neg_fill)
    weights = jnp.exp(logits - jnp.max(logits, axis=1, keepdims=True))
    prob = weights * (1.0 / jnp.sum(weights, axis=1, keepdims=True))
    target = target_ref[mine, :]
    for k in range(nh - 1):
        second[k].wait_recv()
        target = target + target_got[k].astype(jnp.float32)
    slope = loss_weight * (prob - target)
    slope_ref[mine, :] = slope
    part[...] = slope.astype(jnp.bfloat16)
    for k, peer in enumerate(peers):
        third.append(remote(part, got.at[k], ss.at[2, k], rs.at[2, k], {"head": peer}))
        third[-1].start()
    for k, source in enumerate(sources):
        third[k].wait_recv()
        slope_ref[rows_of(source), :] = got[k].astype(jnp.float32)
    for copy in first + second + third:
        copy.wait_send()


def exchange(nh, logits, targets, visible):
    row_count, key_count = logits.shape
    share = row_count // nh
    dma = pltpu.SemaphoreType.DMA
    return pl.pallas_call(
        functools.partial(exchange_kernel, nh),
        out_shape=jax.ShapeDtypeStruct((row_count, key_count), jnp.float32),
        in_specs=[pl.BlockSpec(memory_space=VMEM)] * 3,
        out_specs=pl.BlockSpec(memory_space=VMEM),
        scratch_shapes=[
            VMEM((nh - 1, share, key_count), jnp.float32),
            VMEM((nh - 1, share, key_count), jnp.bfloat16),
            VMEM((row_count, key_count), jnp.bfloat16),
            VMEM((share, key_count), jnp.bfloat16),
            VMEM((nh - 1, share, key_count), jnp.bfloat16),
            dma((3, nh - 1)), dma((3, nh - 1)),
        ],
        compiler_params=pltpu.CompilerParams(collective_id=1, has_side_effects=True),
        name="head_exchange",
    )(logits, targets, visible)


def backward_kernel(idx_ref, w_ref, ik_ref, slope_ref, qgrad_ref, wgrad_ref, kgrad_ref, total):
    rows, gheads, depth = idx_ref.shape
    dot_scale = float(depth) ** (-0.5)
    head_scale = INDEX_HEADS ** (-0.5)
    step = pl.program_id(0)

    @pl.when(step == 0)
    def _():
        total[...] = jnp.zeros_like(total)

    queries = idx_ref[...].reshape(rows * gheads, depth)
    products = lax.dot_general(
        queries, ik_ref[...], (((1,), (1,)), ((), ())), preferred_element_type=jnp.float32
    )
    edges = []
    sums = []
    for r in range(rows):
        p = products[r * gheads : (r + 1) * gheads]
        slope = slope_ref[r : r + 1, :]
        w = w_ref[r * gheads : (r + 1) * gheads, :] * head_scale
        edges.append(jnp.where(p > 0.0, slope * w, 0.0).astype(jnp.bfloat16))
        sums.append(jnp.sum(slope * jnp.maximum(p, 0.0), axis=1, keepdims=True))
    edge = jnp.concatenate(edges, axis=0)
    wgrad_ref[...] = jnp.concatenate(sums, axis=0) * (head_scale * dot_scale)
    qgrad = jnp.dot(edge, ik_ref[...], preferred_element_type=jnp.float32) * dot_scale
    qgrad_ref[...] = qgrad.astype(jnp.bfloat16).reshape(rows, gheads, depth)
    total[...] += lax.dot_general(
        queries, edge, (((0,), (0,)), ((), ())), preferred_element_type=jnp.float32
    )

    @pl.when(step == pl.num_programs(0) - 1)
    def _():
        kgrad_ref[...] = (total[...] * dot_scale).T.astype(jnp.bfloat16)


def backward(index_queries, weights, idx_all, slope, rows=16):
    row_count, gheads, depth = index_queries.shape
    key_count = idx_all.shape[0]
    return pl.pallas_call(
        backward_kernel,
        out_shape=(
            jax.ShapeDtypeStruct((row_count, gheads, depth), jnp.bfloat16),
            jax.ShapeDtypeStruct((row_count * gheads, 1), jnp.float32),
            jax.ShapeDtypeStruct((key_count, depth), jnp.bfloat16),
        ),
        grid=(row_count // rows,),
        in_specs=[
            pl.BlockSpec((rows, gheads, depth), lambda i: (i, 0, 0)),
            pl.BlockSpec((rows * gheads, 1), lambda i: (i, 0)),
            pl.BlockSpec((key_count, depth), lambda i: (0, 0)),
            pl.BlockSpec((rows, key_count), lambda i: (i, 0)),
        ],
        out_specs=(
            pl.BlockSpec((rows, gheads, depth), lambda i: (i, 0, 0)),
            pl.BlockSpec((rows * gheads, 1), lambda i: (i, 0)),
            pl.BlockSpec((key_count, depth), lambda i: (0, 0)),
        ),
        scratch_shapes=[VMEM((depth, key_count), jnp.float32)],
        name="index_backward",
    )(index_queries, weights, idx_all, slope)


def owner_kernel(n, nh, term_ref, out_ref, got, mine, peer, ss, rs, hs, hr):
    me = lax.axis_index("seq")
    head = lax.axis_index("head")
    size = out_ref.shape[0]
    barrier = pltpu.get_barrier_semaphore()
    for k in range(1, n):
        pl.semaphore_signal(barrier, inc=1, device_id={"seq": (me + k) % n}, device_id_type=MESH)
    for k in range(1, nh):
        pl.semaphore_signal(barrier, inc=1, device_id={"head": (head + k) % nh}, device_id_type=MESH)
    pl.semaphore_wait(barrier, n - 1 + nh - 1)
    copies = []
    for k in range(1, n):
        to = (me + k) % n
        copy = remote(
            term_ref.at[pl.ds(pl.multiple_of(to * size, size), size), :],
            got.at[k - 1], ss.at[k - 1], rs.at[k - 1], {"seq": to},
        )
        copy.start()
        copies.append(copy)
    total = term_ref[pl.ds(pl.multiple_of(me * size, size), size), :].astype(jnp.float32)
    for k in range(n - 1):
        copies[k].wait_recv()
        total = total + got[k].astype(jnp.float32)
    mine[...] = total
    last = []
    for k in range(1, nh):
        last.append(remote(mine, peer.at[k - 1], hs.at[k - 1], hr.at[k - 1], {"head": (head + k) % nh}))
        last[-1].start()
    for copy in copies:
        copy.wait_send()
    for k in range(nh - 1):
        last[k].wait_recv()
        total = total + peer[k]
    for copy in last:
        copy.wait_send()
    out_ref[...] = total


def owner_sum(n, nh, term):
    key_count, depth = term.shape
    size = key_count // n
    dma = pltpu.SemaphoreType.DMA
    return pl.pallas_call(
        functools.partial(owner_kernel, n, nh),
        out_shape=jax.ShapeDtypeStruct((size, depth), jnp.float32),
        in_specs=[pl.BlockSpec(memory_space=VMEM)],
        out_specs=pl.BlockSpec(memory_space=VMEM),
        scratch_shapes=[
            VMEM((n - 1, size, depth), jnp.bfloat16),
            VMEM((size, depth), jnp.float32),
            VMEM((nh - 1, size, depth), jnp.float32),
            dma((n - 1,)), dma((n - 1,)), dma((nh - 1,)), dma((nh - 1,)),
        ],
        compiler_params=pltpu.CompilerParams(collective_id=2, has_side_effects=True),
        name="owner_sum",
    )(term)


def body(n, nh, latent_queries, latent_keys, index_queries, index_keys, head_weights, visible):
    row_count, gheads = head_weights.shape
    weights = head_weights.reshape(row_count * gheads, 1)
    lat_all, idx_all = gather_keys(n, latent_keys, index_keys)
    logits, targets = forward(latent_queries, index_queries, weights, visible, lat_all, idx_all)
    slope = exchange(nh, logits, targets, visible.reshape(row_count, 1))
    query_grad, weight_grad, term = backward(index_queries, weights, idx_all, slope)
    key_grad = owner_sum(n, nh, term)
    return query_grad, weight_grad.reshape(row_count, gheads), key_grad


def solution(mesh):
    placed = (
        P("seq", "head", None),
        P("seq", None),
        P("seq", "head", None),
        P("seq", None),
        P("seq", "head"),
        P("seq"),
    )
    return jax.shard_map(
        functools.partial(body, mesh.shape["seq"], mesh.shape["head"]),
        mesh=mesh,
        in_specs=placed,
        out_specs=(P("seq", "head", None), P("seq", "head"), P("seq", None)),
        check_vma=False,
    )
```

```python
import functools
import jax
import jax.numpy as jnp
from jax import lax
from jax.experimental import pallas as pl
from jax.experimental.pallas import tpu as pltpu
from jax.sharding import PartitionSpec as P

MLA_HEADS = 128
INDEX_HEADS = 64
LOG2E = 1.4426950408889634

mla_scale = 192.0 ** (-0.5)
loss_weight = 16.0
neg_fill = -1e30
MESH = pl.DeviceIdType.MESH
VMEM = pltpu.VMEM


def line_sizes(n):
    ny = 2 if n <= 16 else 4
    return n // (2 * ny), ny


def remote(src, dst, ssem, rsem, device):
    return pltpu.make_async_remote_copy(
        src_ref=src, dst_ref=dst, send_sem=ssem, recv_sem=rsem, device_id=device, device_id_type=MESH
    )


def gather_kernel(n, lat_ref, idx_ref, lat_all, idx_all, lsem, zs, zr, ys, yr, cs, cr):
    nz, ny = line_sizes(n)
    me = lax.axis_index("seq")
    core = me % 2
    y = (me // 2) % ny
    z = me // (2 * ny)
    size = lat_ref.shape[0]

    def at(zz, yy, cc):
        return (zz * ny + yy) * 2 + cc

    zpeers = [(z + k) % nz for k in range(1, nz)]
    ypeers = [(y + k) % ny for k in range(1, ny)]
    barrier = pltpu.get_barrier_semaphore()
    for zz in zpeers:
        pl.semaphore_signal(barrier, inc=1, device_id={"seq": at(zz, y, core)}, device_id_type=MESH)
    for yy in ypeers:
        pl.semaphore_signal(barrier, inc=1, device_id={"seq": at(z, yy, core)}, device_id_type=MESH)
    pl.semaphore_signal(barrier, inc=1, device_id={"seq": at(z, y, 1 - core)}, device_id_type=MESH)

    def rows(ref, owner):
        return ref.at[pl.ds(pl.multiple_of(owner * size, size), size), :]

    locals_ = [
        pltpu.make_async_copy(lat_ref, rows(lat_all, me), lsem.at[0]),
        pltpu.make_async_copy(idx_ref, rows(idx_all, me), lsem.at[1]),
    ]
    for c in locals_:
        c.start()
    pl.semaphore_wait(barrier, nz - 1 + ny - 1 + 1)
    pending = []

    def send(owner, device, ssem, rsem, first):
        src_l = lat_ref if first else rows(lat_all, owner)
        src_i = idx_ref if first else rows(idx_all, owner)
        out = [
            remote(src_l, rows(lat_all, owner), ssem.at[0], rsem.at[0], {"seq": device}),
            remote(src_i, rows(idx_all, owner), ssem.at[1], rsem.at[1], {"seq": device}),
        ]
        for c in out:
            c.start()
        pending.extend(out)

    def receive(owner, sems, rsem):
        remote(lat_ref, rows(lat_all, owner), sems.at[0], rsem.at[0], {"seq": me}).wait_recv()
        remote(idx_ref, rows(idx_all, owner), sems.at[1], rsem.at[1], {"seq": me}).wait_recv()

    for k in range(1, nz):
        send(me, at((z + k) % nz, y, core), zs.at[k], zr.at[k], True)
    for j in range(1, ny):
        send(me, at(z, (y + j) % ny, core), ys.at[0, j], yr.at[0, j], True)
    send(me, at(z, y, 1 - core), cs.at[0, 0], cr.at[0, 0], True)
    for k in range(1, nz):
        owner = at((z - k + nz) % nz, y, core)
        receive(owner, zs.at[k], zr.at[k])
        for j in range(1, ny):
            send(owner, at(z, (y + j) % ny, core), ys.at[k, j], yr.at[k, j], False)
        send(owner, at(z, y, 1 - core), cs.at[k, 0], cr.at[k, 0], False)
    for k in range(nz):
        for j in range(1, ny):
            owner = at((z - k + nz) % nz, (y - j + ny) % ny, core)
            receive(owner, ys.at[k, j], yr.at[k, j])
            send(owner, at(z, y, 1 - core), cs.at[k, j], cr.at[k, j], False)
    for k in range(nz):
        for j in range(ny):
            owner = at((z - k + nz) % nz, (y - j + ny) % ny, 1 - core)
            receive(owner, cs.at[k, j], cr.at[k, j])
    for c in pending:
        c.wait_send()
    for c in locals_:
        c.wait()


def gather_keys(n, latent_keys, index_keys):
    nz, ny = line_sizes(n)
    size, width = latent_keys.shape
    depth = index_keys.shape[1]
    dma = pltpu.SemaphoreType.DMA
    return pl.pallas_call(
        functools.partial(gather_kernel, n),
        out_shape=(
            jax.ShapeDtypeStruct((n * size, width), jnp.bfloat16),
            jax.ShapeDtypeStruct((n * size, depth), jnp.bfloat16),
        ),
        in_specs=[pl.BlockSpec(memory_space=VMEM)] * 2,
        out_specs=(pl.BlockSpec(memory_space=VMEM),) * 2,
        scratch_shapes=[
            dma((2,)),
            dma((nz, 2)), dma((nz, 2)),
            dma((nz, ny, 2)), dma((nz, ny, 2)),
            dma((nz, ny, 2)), dma((nz, ny, 2)),
        ],
        compiler_params=pltpu.CompilerParams(collective_id=0, has_side_effects=True),
        name="gather_keys",
    )(latent_keys, index_keys)


def forward_kernel(
    vis_ref, lat_ref, idx_ref, w_ref, lk_ref, ik_ref, logit_ref, target_ref, split_ref, wide, bias, total
):
    block, width, row_count = lat_ref.shape
    gheads = w_ref.shape[0]
    key_count = lk_ref.shape[0]
    depth = ik_ref.shape[1]
    step = pl.program_id(0)
    c = mla_scale * LOG2E

    @pl.when(step == 0)
    def _():
        ids = lax.broadcasted_iota(jnp.int32, (key_count, row_count), 0)
        bias[...] = jnp.where(ids < vis_ref[...], 0.0, neg_fill)
        wide[...] = idx_ref[...].astype(jnp.float32)
        total[...] = jnp.zeros_like(total)
        scale = float(depth) ** (-0.5) * INDEX_HEADS ** (-0.5)

        def pair(number, _):
            g = number * 2
            parts = [wide[pl.ds(g + j, row_count, stride=gheads), :].astype(jnp.bfloat16) for j in range(2)]
            for j in range(2):
                split_ref[g + j] = parts[j]
            products = lax.dot_general(
                ik_ref[...], jnp.concatenate(parts, axis=0), (((1,), (1,)), ((), ())),
                preferred_element_type=jnp.float32,
            )
            w = w_ref[pl.ds(g, 2), :] * scale
            total[...] += (
                jnp.maximum(products[:, :row_count], 0.0) * w[0:1]
                + jnp.maximum(products[:, row_count:], 0.0) * w[1:2]
            )
            return 0

        lax.fori_loop(0, gheads // 2, pair, 0)
        logit_ref[...] = total[...].T
        total[...] = jnp.zeros_like(total)

    def scores_of(j):
        queries = jnp.concatenate([lat_ref[2 * j], lat_ref[2 * j + 1]], axis=1)
        return jnp.dot(lk_ref[...], queries, preferred_element_type=jnp.float32)

    scores = scores_of(0)
    for j in range(block // 2):
        following = scores_of(j + 1) if j + 1 < block // 2 else None
        added = None
        for part in range(2):
            s = scores[:, part * row_count : (part + 1) * row_count] + bias[...]
            peak = jnp.max(s, axis=0, keepdims=True)
            e = jnp.exp2((s - peak) * c)
            term = e * ((1.0 / MLA_HEADS) / jnp.sum(e, axis=0, keepdims=True))
            added = term if added is None else added + term
        total[...] += added
        scores = following

    @pl.when(step == pl.num_programs(0) - 1)
    def _():
        target_ref[...] = total[...].T


def forward(latent_t, index_flat, weights_t, visible, lat_all, idx_all, block=8):
    heads, width, row_count = latent_t.shape
    gheads = weights_t.shape[0]
    key_count, depth = idx_all.shape
    whole = lambda *shape: pl.BlockSpec(shape, lambda i: (0,) * len(shape))
    return pl.pallas_call(
        forward_kernel,
        out_shape=(
            jax.ShapeDtypeStruct((row_count, key_count), jnp.float32),
            jax.ShapeDtypeStruct((row_count, key_count), jnp.float32),
            jax.ShapeDtypeStruct((gheads, row_count, depth), jnp.bfloat16),
        ),
        grid=(heads // block,),
        in_specs=[
            whole(1, row_count),
            pl.BlockSpec((block, width, row_count), lambda i: (i, 0, 0)),
            whole(row_count * gheads, depth),
            whole(gheads, row_count),
            whole(key_count, width),
            whole(key_count, depth),
        ],
        out_specs=(
            whole(row_count, key_count),
            whole(row_count, key_count),
            whole(gheads, row_count, depth),
        ),
        scratch_shapes=[
            VMEM((row_count * gheads, depth), jnp.float32),
            VMEM((key_count, row_count), jnp.float32),
            VMEM((key_count, row_count), jnp.float32),
        ],
        name="forward_rows",
    )(visible, latent_t, index_flat, weights_t, lat_all, idx_all)


def exchange_kernel(nh, logit_ref, target_ref, vis_ref, slope_ref, logit_got, target_got, target_out, part, got, ss, rs):
    me = lax.axis_index("head")
    share = logit_ref.shape[0] // nh

    def rows_of(owner):
        return pl.ds(pl.multiple_of(owner * share, share), share)

    mine = rows_of(me)
    peers = [(me + k) % nh for k in range(1, nh)]
    sources = [(me - k + nh) % nh for k in range(1, nh)]
    barrier = pltpu.get_barrier_semaphore()
    for peer in peers:
        pl.semaphore_signal(barrier, inc=1, device_id={"head": peer}, device_id_type=MESH)
    target_out[...] = target_ref[...].astype(jnp.bfloat16)
    pl.semaphore_wait(barrier, nh - 1)
    first, second, third = [], [], []
    for k, peer in enumerate(peers):
        first.append(remote(logit_ref.at[rows_of(peer), :], logit_got.at[k], ss.at[0, k], rs.at[0, k], {"head": peer}))
        first[-1].start()
    for k, peer in enumerate(peers):
        second.append(remote(target_out.at[rows_of(peer), :], target_got.at[k], ss.at[1, k], rs.at[1, k], {"head": peer}))
        second[-1].start()
    logits = logit_ref[mine, :]
    for k in range(nh - 1):
        first[k].wait_recv()
        logits = logits + logit_got[k]
    ids = lax.broadcasted_iota(jnp.int32, logits.shape, 1)
    logits = jnp.where(ids < vis_ref[mine, :], logits, neg_fill)
    weights = jnp.exp(logits - jnp.max(logits, axis=1, keepdims=True))
    prob = weights * (1.0 / jnp.sum(weights, axis=1, keepdims=True))
    target = target_ref[mine, :]
    for k in range(nh - 1):
        second[k].wait_recv()
        target = target + target_got[k].astype(jnp.float32)
    slope = loss_weight * (prob - target)
    slope_ref[mine, :] = slope
    part[...] = slope.astype(jnp.bfloat16)
    for k, peer in enumerate(peers):
        third.append(remote(part, got.at[k], ss.at[2, k], rs.at[2, k], {"head": peer}))
        third[-1].start()
    for k, source in enumerate(sources):
        third[k].wait_recv()
        slope_ref[rows_of(source), :] = got[k].astype(jnp.float32)
    for copy in first + second + third:
        copy.wait_send()


def exchange(nh, logits, targets, visible):
    row_count, key_count = logits.shape
    share = row_count // nh
    dma = pltpu.SemaphoreType.DMA
    return pl.pallas_call(
        functools.partial(exchange_kernel, nh),
        out_shape=jax.ShapeDtypeStruct((row_count, key_count), jnp.float32),
        in_specs=[pl.BlockSpec(memory_space=VMEM)] * 3,
        out_specs=pl.BlockSpec(memory_space=VMEM),
        scratch_shapes=[
            VMEM((nh - 1, share, key_count), jnp.float32),
            VMEM((nh - 1, share, key_count), jnp.bfloat16),
            VMEM((row_count, key_count), jnp.bfloat16),
            VMEM((share, key_count), jnp.bfloat16),
            VMEM((nh - 1, share, key_count), jnp.bfloat16),
            dma((3, nh - 1)), dma((3, nh - 1)),
        ],
        compiler_params=pltpu.CompilerParams(collective_id=1, has_side_effects=True),
        name="head_exchange",
    )(logits, targets, visible)


def backward_kernel(split_ref, w_ref, ik_ref, slope_ref, qgrad_ref, wgrad_ref, kgrad_ref, slope, ikt, total, wide):
    block, row_count, depth = split_ref.shape
    gheads = wide.shape[0] // row_count
    dot_scale = float(depth) ** (-0.5)
    head_scale = INDEX_HEADS ** (-0.5)
    step = pl.program_id(0)

    @pl.when(step == 0)
    def _():
        total[...] = jnp.zeros_like(total)
        slope[...] = slope_ref[...].T
        ikt[...] = ik_ref[...].astype(jnp.float32).T.astype(jnp.bfloat16)

    w = w_ref[...] * head_scale
    sums = []
    for j in range(block // 2):
        queries = split_ref[2 * j : 2 * j + 2].reshape(2 * row_count, depth)
        products = lax.dot_general(
            ik_ref[...], queries, (((1,), (1,)), ((), ())), preferred_element_type=jnp.float32
        )
        edges = []
        for part in range(2):
            p = products[:, part * row_count : (part + 1) * row_count]
            g = 2 * j + part
            edges.append(jnp.where(p > 0.0, slope[...] * w[g : g + 1], 0.0).astype(jnp.bfloat16))
            sums.append(jnp.sum(slope[...] * jnp.maximum(p, 0.0), axis=0, keepdims=True))
        edge = jnp.concatenate(edges, axis=1)
        total[...] += jnp.dot(edge, queries, preferred_element_type=jnp.float32)
        qgrad = (jnp.dot(ikt[...], edge, preferred_element_type=jnp.float32) * dot_scale).T
        for part in range(2):
            wide[pl.ds(step * block + 2 * j + part, row_count, stride=gheads), :] = qgrad[
                part * row_count : (part + 1) * row_count
            ]
    wgrad_ref[...] = jnp.concatenate(sums, axis=0) * (head_scale * dot_scale)

    @pl.when(step == pl.num_programs(0) - 1)
    def _():
        kgrad_ref[...] = (total[...] * dot_scale).astype(jnp.bfloat16)
        qgrad_ref[...] = wide[...].astype(jnp.bfloat16)


def backward(split, weights_t, idx_all, slope, block=8):
    gheads, row_count, depth = split.shape
    key_count = idx_all.shape[0]
    whole = lambda *shape: pl.BlockSpec(shape, lambda i: (0,) * len(shape))
    return pl.pallas_call(
        backward_kernel,
        out_shape=(
            jax.ShapeDtypeStruct((row_count * gheads, depth), jnp.bfloat16),
            jax.ShapeDtypeStruct((gheads, row_count), jnp.float32),
            jax.ShapeDtypeStruct((key_count, depth), jnp.bfloat16),
        ),
        grid=(gheads // block,),
        in_specs=[
            pl.BlockSpec((block, row_count, depth), lambda i: (i, 0, 0)),
            pl.BlockSpec((block, row_count), lambda i: (i, 0)),
            whole(key_count, depth),
            whole(row_count, key_count),
        ],
        out_specs=(
            whole(row_count * gheads, depth),
            pl.BlockSpec((block, row_count), lambda i: (i, 0)),
            whole(key_count, depth),
        ),
        scratch_shapes=[
            VMEM((key_count, row_count), jnp.float32),
            VMEM((depth, key_count), jnp.bfloat16),
            VMEM((key_count, depth), jnp.float32),
            VMEM((row_count * gheads, depth), jnp.float32),
        ],
        name="index_backward",
    )(split, weights_t, idx_all, slope)


def owner_kernel(n, nh, term_ref, out_ref, got, mine, peer, ss, rs, hs, hr):
    me = lax.axis_index("seq")
    head = lax.axis_index("head")
    size = out_ref.shape[0]
    barrier = pltpu.get_barrier_semaphore()
    for k in range(1, n):
        pl.semaphore_signal(barrier, inc=1, device_id={"seq": (me + k) % n}, device_id_type=MESH)
    for k in range(1, nh):
        pl.semaphore_signal(barrier, inc=1, device_id={"head": (head + k) % nh}, device_id_type=MESH)
    pl.semaphore_wait(barrier, n - 1 + nh - 1)
    copies = []
    for k in range(1, n):
        to = (me + k) % n
        copy = remote(
            term_ref.at[pl.ds(pl.multiple_of(to * size, size), size), :],
            got.at[k - 1], ss.at[k - 1], rs.at[k - 1], {"seq": to},
        )
        copy.start()
        copies.append(copy)
    total = term_ref[pl.ds(pl.multiple_of(me * size, size), size), :].astype(jnp.float32)
    for k in range(n - 1):
        copies[k].wait_recv()
        total = total + got[k].astype(jnp.float32)
    mine[...] = total
    last = []
    for k in range(1, nh):
        last.append(remote(mine, peer.at[k - 1], hs.at[k - 1], hr.at[k - 1], {"head": (head + k) % nh}))
        last[-1].start()
    for copy in copies:
        copy.wait_send()
    for k in range(nh - 1):
        last[k].wait_recv()
        total = total + peer[k]
    for copy in last:
        copy.wait_send()
    out_ref[...] = total


def owner_sum(n, nh, term):
    key_count, depth = term.shape
    size = key_count // n
    dma = pltpu.SemaphoreType.DMA
    return pl.pallas_call(
        functools.partial(owner_kernel, n, nh),
        out_shape=jax.ShapeDtypeStruct((size, depth), jnp.float32),
        in_specs=[pl.BlockSpec(memory_space=VMEM)],
        out_specs=pl.BlockSpec(memory_space=VMEM),
        scratch_shapes=[
            VMEM((n - 1, size, depth), jnp.bfloat16),
            VMEM((size, depth), jnp.float32),
            VMEM((nh - 1, size, depth), jnp.float32),
            dma((n - 1,)), dma((n - 1,)), dma((nh - 1,)), dma((nh - 1,)),
        ],
        compiler_params=pltpu.CompilerParams(collective_id=2, has_side_effects=True),
        name="owner_sum",
    )(term)


def body(n, nh, latent_queries, latent_keys, index_queries, index_keys, head_weights, visible):
    row_count, gheads, depth = index_queries.shape
    weights_t = head_weights.T
    lat_all, idx_all = gather_keys(n, latent_keys, index_keys)
    logits, targets, split = forward(
        jnp.transpose(latent_queries, (1, 2, 0)),
        index_queries.reshape(row_count * gheads, depth),
        weights_t,
        visible.reshape(1, row_count),
        lat_all,
        idx_all,
    )
    slope = exchange(nh, logits, targets, visible.reshape(row_count, 1))
    query_grad, weight_grad, term = backward(split, weights_t, idx_all, slope)
    key_grad = owner_sum(n, nh, term)
    return query_grad.reshape(row_count, gheads, depth), weight_grad.T, key_grad


def solution(mesh):
    placed = (
        P("seq", "head", None),
        P("seq", None),
        P("seq", "head", None),
        P("seq", None),
        P("seq", "head"),
        P("seq"),
    )
    return jax.shard_map(
        functools.partial(body, mesh.shape["seq"], mesh.shape["head"]),
        mesh=mesh,
        in_specs=placed,
        out_specs=(P("seq", "head", None), P("seq", "head"), P("seq", None)),
        check_vma=False,
    )
```

```python
import functools
import jax
import jax.numpy as jnp
from jax import lax
from jax.experimental import pallas as pl
from jax.experimental.pallas import tpu as pltpu
from jax.sharding import PartitionSpec as P

MLA_HEADS = 128
INDEX_HEADS = 64
LOG2E = 1.4426950408889634

mla_scale = 192.0 ** (-0.5)
loss_weight = 16.0
neg_fill = -1e30
MESH = pl.DeviceIdType.MESH
VMEM = pltpu.VMEM


def line_sizes(n):
    ny = 2 if n <= 16 else 4
    return n // (2 * ny), ny


def remote(src, dst, ssem, rsem, device):
    return pltpu.make_async_remote_copy(
        src_ref=src, dst_ref=dst, send_sem=ssem, recv_sem=rsem, device_id=device, device_id_type=MESH
    )


def gather_kernel(n, lat_ref, idx_ref, lat_all, idx_all, lsem, zs, zr, ys, yr, cs, cr):
    nz, ny = line_sizes(n)
    me = lax.axis_index("seq")
    core = me % 2
    y = (me // 2) % ny
    z = me // (2 * ny)
    size = lat_ref.shape[0]

    def at(zz, yy, cc):
        return (zz * ny + yy) * 2 + cc

    zpeers = [(z + k) % nz for k in range(1, nz)]
    ypeers = [(y + k) % ny for k in range(1, ny)]
    barrier = pltpu.get_barrier_semaphore()
    for zz in zpeers:
        pl.semaphore_signal(barrier, inc=1, device_id={"seq": at(zz, y, core)}, device_id_type=MESH)
    for yy in ypeers:
        pl.semaphore_signal(barrier, inc=1, device_id={"seq": at(z, yy, core)}, device_id_type=MESH)
    pl.semaphore_signal(barrier, inc=1, device_id={"seq": at(z, y, 1 - core)}, device_id_type=MESH)

    def rows(ref, owner):
        return ref.at[pl.ds(pl.multiple_of(owner * size, size), size), :]

    locals_ = [
        pltpu.make_async_copy(lat_ref, rows(lat_all, me), lsem.at[0]),
        pltpu.make_async_copy(idx_ref, rows(idx_all, me), lsem.at[1]),
    ]
    for c in locals_:
        c.start()
    pl.semaphore_wait(barrier, nz - 1 + ny - 1 + 1)
    pending = []

    def send(owner, device, ssem, rsem, first):
        src_l = lat_ref if first else rows(lat_all, owner)
        src_i = idx_ref if first else rows(idx_all, owner)
        out = [
            remote(src_l, rows(lat_all, owner), ssem.at[0], rsem.at[0], {"seq": device}),
            remote(src_i, rows(idx_all, owner), ssem.at[1], rsem.at[1], {"seq": device}),
        ]
        for c in out:
            c.start()
        pending.extend(out)

    def receive(owner, sems, rsem):
        remote(lat_ref, rows(lat_all, owner), sems.at[0], rsem.at[0], {"seq": me}).wait_recv()
        remote(idx_ref, rows(idx_all, owner), sems.at[1], rsem.at[1], {"seq": me}).wait_recv()

    for k in range(1, nz):
        send(me, at((z + k) % nz, y, core), zs.at[k], zr.at[k], True)
    for j in range(1, ny):
        send(me, at(z, (y + j) % ny, core), ys.at[0, j], yr.at[0, j], True)
    send(me, at(z, y, 1 - core), cs.at[0, 0], cr.at[0, 0], True)
    for k in range(1, nz):
        owner = at((z - k + nz) % nz, y, core)
        receive(owner, zs.at[k], zr.at[k])
        for j in range(1, ny):
            send(owner, at(z, (y + j) % ny, core), ys.at[k, j], yr.at[k, j], False)
        send(owner, at(z, y, 1 - core), cs.at[k, 0], cr.at[k, 0], False)
    for k in range(nz):
        for j in range(1, ny):
            owner = at((z - k + nz) % nz, (y - j + ny) % ny, core)
            receive(owner, ys.at[k, j], yr.at[k, j])
            send(owner, at(z, y, 1 - core), cs.at[k, j], cr.at[k, j], False)
    for k in range(nz):
        for j in range(ny):
            owner = at((z - k + nz) % nz, (y - j + ny) % ny, 1 - core)
            receive(owner, cs.at[k, j], cr.at[k, j])
    for c in pending:
        c.wait_send()
    for c in locals_:
        c.wait()


def gather_keys(n, latent_keys, index_keys):
    nz, ny = line_sizes(n)
    size, width = latent_keys.shape
    depth = index_keys.shape[1]
    dma = pltpu.SemaphoreType.DMA
    return pl.pallas_call(
        functools.partial(gather_kernel, n),
        out_shape=(
            jax.ShapeDtypeStruct((n * size, width), jnp.bfloat16),
            jax.ShapeDtypeStruct((n * size, depth), jnp.bfloat16),
        ),
        in_specs=[pl.BlockSpec(memory_space=VMEM)] * 2,
        out_specs=(pl.BlockSpec(memory_space=VMEM),) * 2,
        scratch_shapes=[
            dma((2,)),
            dma((nz, 2)), dma((nz, 2)),
            dma((nz, ny, 2)), dma((nz, ny, 2)),
            dma((nz, ny, 2)), dma((nz, ny, 2)),
        ],
        compiler_params=pltpu.CompilerParams(collective_id=0, has_side_effects=True),
        name="gather_keys",
    )(latent_keys, index_keys)


def logits_kernel(idx_ref, w_ref, ik_ref, logit_ref, split_ref, wide, total):
    gheads, row_count = w_ref.shape
    depth = ik_ref.shape[1]
    wide[...] = idx_ref[...].astype(jnp.float32)
    total[...] = jnp.zeros_like(total)
    scale = float(depth) ** (-0.5) * INDEX_HEADS ** (-0.5)

    def pair(number, _):
        g = number * 2
        parts = [wide[pl.ds(g + j, row_count, stride=gheads), :].astype(jnp.bfloat16) for j in range(2)]
        for j in range(2):
            split_ref[g + j] = parts[j]
        products = lax.dot_general(
            ik_ref[...], jnp.concatenate(parts, axis=0), (((1,), (1,)), ((), ())),
            preferred_element_type=jnp.float32,
        )
        w = w_ref[pl.ds(g, 2), :] * scale
        total[...] += (
            jnp.maximum(products[:, :row_count], 0.0) * w[0:1]
            + jnp.maximum(products[:, row_count:], 0.0) * w[1:2]
        )
        return 0

    lax.fori_loop(0, gheads // 2, pair, 0)
    logit_ref[...] = total[...].T


def index_forward(index_flat, weights_t, idx_all):
    gheads, row_count = weights_t.shape
    key_count, depth = idx_all.shape
    return pl.pallas_call(
        logits_kernel,
        out_shape=(
            jax.ShapeDtypeStruct((row_count, key_count), jnp.float32),
            jax.ShapeDtypeStruct((gheads, row_count, depth), jnp.bfloat16),
        ),
        in_specs=[pl.BlockSpec(memory_space=VMEM)] * 3,
        out_specs=(pl.BlockSpec(memory_space=VMEM),) * 2,
        scratch_shapes=[
            VMEM((row_count * gheads, depth), jnp.float32),
            VMEM((key_count, row_count), jnp.float32),
        ],
        name="index_forward",
    )(index_flat, weights_t, idx_all)


def forward_kernel(vis_ref, lat_ref, lk_ref, target_ref, bias, total):
    block, width, row_count = lat_ref.shape
    key_count = lk_ref.shape[0]
    step = pl.program_id(0)
    c = mla_scale * LOG2E

    @pl.when(step == 0)
    def _():
        ids = lax.broadcasted_iota(jnp.int32, (key_count, row_count), 0)
        bias[...] = jnp.where(ids < vis_ref[...], 0.0, neg_fill)
        total[...] = jnp.zeros_like(total)

    def scores_of(j):
        queries = jnp.concatenate([lat_ref[2 * j], lat_ref[2 * j + 1]], axis=1)
        return jnp.dot(lk_ref[...], queries, preferred_element_type=jnp.float32)

    scores = scores_of(0)
    for j in range(block // 2):
        following = scores_of(j + 1) if j + 1 < block // 2 else None
        added = None
        for part in range(2):
            s = scores[:, part * row_count : (part + 1) * row_count] + bias[...]
            peak = jnp.max(s, axis=0, keepdims=True)
            e = jnp.exp2((s - peak) * c)
            term = e * ((1.0 / MLA_HEADS) / jnp.sum(e, axis=0, keepdims=True))
            added = term if added is None else added + term
        total[...] += added
        scores = following

    @pl.when(step == pl.num_programs(0) - 1)
    def _():
        target_ref[...] = total[...].T


def forward(latent_t, visible, lat_all, block=8):
    heads, width, row_count = latent_t.shape
    key_count = lat_all.shape[0]
    whole = lambda *shape: pl.BlockSpec(shape, lambda i: (0,) * len(shape))
    return pl.pallas_call(
        forward_kernel,
        out_shape=jax.ShapeDtypeStruct((row_count, key_count), jnp.float32),
        grid=(heads // block,),
        in_specs=[
            whole(1, row_count),
            pl.BlockSpec((block, width, row_count), lambda i: (i, 0, 0)),
            whole(key_count, width),
        ],
        out_specs=whole(row_count, key_count),
        scratch_shapes=[
            VMEM((key_count, row_count), jnp.float32),
            VMEM((key_count, row_count), jnp.float32),
        ],
        cost_estimate=pl.CostEstimate(
            flops=2 * heads * width * row_count * key_count,
            bytes_accessed=2 * heads * width * row_count,
            transcendentals=heads * row_count * key_count,
        ),
        name="latent_forward",
    )(visible, latent_t, lat_all)


def exchange_kernel(nh, logit_ref, target_ref, vis_ref, slope_ref, target_got, target_out, part, got, ss, rs):
    me = lax.axis_index("head")
    share = logit_ref.shape[0]

    def rows_of(owner):
        return pl.ds(pl.multiple_of(owner * share, share), share)

    mine = rows_of(me)
    peers = [(me + k) % nh for k in range(1, nh)]
    sources = [(me - k + nh) % nh for k in range(1, nh)]
    barrier = pltpu.get_barrier_semaphore()
    for peer in peers:
        pl.semaphore_signal(barrier, inc=1, device_id={"head": peer}, device_id_type=MESH)
    target_out[...] = target_ref[...].astype(jnp.bfloat16)
    pl.semaphore_wait(barrier, nh - 1)
    second, third = [], []
    for k, peer in enumerate(peers):
        second.append(remote(target_out.at[rows_of(peer), :], target_got.at[k], ss.at[1, k], rs.at[1, k], {"head": peer}))
        second[-1].start()
    logits = logit_ref[...]
    ids = lax.broadcasted_iota(jnp.int32, logits.shape, 1)
    logits = jnp.where(ids < vis_ref[mine, :], logits, neg_fill)
    weights = jnp.exp(logits - jnp.max(logits, axis=1, keepdims=True))
    prob = weights * (1.0 / jnp.sum(weights, axis=1, keepdims=True))
    target = target_ref[mine, :]
    for k in range(nh - 1):
        second[k].wait_recv()
        target = target + target_got[k].astype(jnp.float32)
    slope = loss_weight * (prob - target)
    slope_ref[mine, :] = slope
    part[...] = slope.astype(jnp.bfloat16)
    for k, peer in enumerate(peers):
        third.append(remote(part, got.at[k], ss.at[2, k], rs.at[2, k], {"head": peer}))
        third[-1].start()
    for k, source in enumerate(sources):
        third[k].wait_recv()
        slope_ref[rows_of(source), :] = got[k].astype(jnp.float32)
    for copy in second + third:
        copy.wait_send()


def exchange(nh, logits, targets, visible):
    row_count, key_count = targets.shape
    share = row_count // nh
    dma = pltpu.SemaphoreType.DMA
    return pl.pallas_call(
        functools.partial(exchange_kernel, nh),
        out_shape=jax.ShapeDtypeStruct((row_count, key_count), jnp.float32),
        in_specs=[pl.BlockSpec(memory_space=VMEM)] * 3,
        out_specs=pl.BlockSpec(memory_space=VMEM),
        scratch_shapes=[
            VMEM((nh - 1, share, key_count), jnp.bfloat16),
            VMEM((row_count, key_count), jnp.bfloat16),
            VMEM((share, key_count), jnp.bfloat16),
            VMEM((nh - 1, share, key_count), jnp.bfloat16),
            dma((3, nh - 1)), dma((3, nh - 1)),
        ],
        compiler_params=pltpu.CompilerParams(collective_id=1, has_side_effects=True),
        name="head_exchange",
    )(logits, targets, visible)


def backward_kernel(split_ref, w_ref, ik_ref, slope_ref, qgrad_ref, wgrad_ref, kgrad_ref, slope, ikt, total, wide):
    block, row_count, depth = split_ref.shape
    gheads = wide.shape[0] // row_count
    dot_scale = float(depth) ** (-0.5)
    head_scale = INDEX_HEADS ** (-0.5)
    step = pl.program_id(0)

    @pl.when(step == 0)
    def _():
        total[...] = jnp.zeros_like(total)
        slope[...] = slope_ref[...].T
        ikt[...] = ik_ref[...].astype(jnp.float32).T.astype(jnp.bfloat16)

    w = w_ref[...] * head_scale
    sums = []
    for j in range(block // 2):
        queries = split_ref[2 * j : 2 * j + 2].reshape(2 * row_count, depth)
        products = lax.dot_general(
            ik_ref[...], queries, (((1,), (1,)), ((), ())), preferred_element_type=jnp.float32
        )
        edges = []
        for part in range(2):
            p = products[:, part * row_count : (part + 1) * row_count]
            g = 2 * j + part
            edges.append(jnp.where(p > 0.0, slope[...] * w[g : g + 1], 0.0).astype(jnp.bfloat16))
            sums.append(jnp.sum(slope[...] * jnp.maximum(p, 0.0), axis=0, keepdims=True))
        edge = jnp.concatenate(edges, axis=1)
        total[...] += jnp.dot(edge, queries, preferred_element_type=jnp.float32)
        qgrad = (jnp.dot(ikt[...], edge, preferred_element_type=jnp.float32) * dot_scale).T
        for part in range(2):
            wide[pl.ds(step * block + 2 * j + part, row_count, stride=gheads), :] = qgrad[
                part * row_count : (part + 1) * row_count
            ]
    wgrad_ref[...] = jnp.concatenate(sums, axis=0) * (head_scale * dot_scale)

    @pl.when(step == pl.num_programs(0) - 1)
    def _():
        kgrad_ref[...] = (total[...] * dot_scale).astype(jnp.bfloat16)
        qgrad_ref[...] = wide[...].astype(jnp.bfloat16)


def backward(split, weights_t, idx_all, slope, block=8):
    gheads, row_count, depth = split.shape
    key_count = idx_all.shape[0]
    whole = lambda *shape: pl.BlockSpec(shape, lambda i: (0,) * len(shape))
    return pl.pallas_call(
        backward_kernel,
        out_shape=(
            jax.ShapeDtypeStruct((row_count * gheads, depth), jnp.bfloat16),
            jax.ShapeDtypeStruct((gheads, row_count), jnp.float32),
            jax.ShapeDtypeStruct((key_count, depth), jnp.bfloat16),
        ),
        grid=(gheads // block,),
        in_specs=[
            pl.BlockSpec((block, row_count, depth), lambda i: (i, 0, 0)),
            pl.BlockSpec((block, row_count), lambda i: (i, 0)),
            whole(key_count, depth),
            whole(row_count, key_count),
        ],
        out_specs=(
            whole(row_count * gheads, depth),
            pl.BlockSpec((block, row_count), lambda i: (i, 0)),
            whole(key_count, depth),
        ),
        scratch_shapes=[
            VMEM((key_count, row_count), jnp.float32),
            VMEM((depth, key_count), jnp.bfloat16),
            VMEM((key_count, depth), jnp.float32),
            VMEM((row_count * gheads, depth), jnp.float32),
        ],
        name="index_backward",
    )(split, weights_t, idx_all, slope)


def owner_kernel(n, nh, term_ref, out_ref, got, mine, peer, ss, rs, hs, hr):
    me = lax.axis_index("seq")
    head = lax.axis_index("head")
    size = out_ref.shape[0]
    barrier = pltpu.get_barrier_semaphore()
    for k in range(1, n):
        pl.semaphore_signal(barrier, inc=1, device_id={"seq": (me + k) % n}, device_id_type=MESH)
    for k in range(1, nh):
        pl.semaphore_signal(barrier, inc=1, device_id={"head": (head + k) % nh}, device_id_type=MESH)
    pl.semaphore_wait(barrier, n - 1 + nh - 1)
    copies = []
    for k in range(1, n):
        to = (me + k) % n
        copy = remote(
            term_ref.at[pl.ds(pl.multiple_of(to * size, size), size), :],
            got.at[k - 1], ss.at[k - 1], rs.at[k - 1], {"seq": to},
        )
        copy.start()
        copies.append(copy)
    total = term_ref[pl.ds(pl.multiple_of(me * size, size), size), :].astype(jnp.float32)
    for k in range(n - 1):
        copies[k].wait_recv()
        total = total + got[k].astype(jnp.float32)
    mine[...] = total
    last = []
    for k in range(1, nh):
        last.append(remote(mine, peer.at[k - 1], hs.at[k - 1], hr.at[k - 1], {"head": (head + k) % nh}))
        last[-1].start()
    for copy in copies:
        copy.wait_send()
    for k in range(nh - 1):
        last[k].wait_recv()
        total = total + peer[k]
    for copy in last:
        copy.wait_send()
    out_ref[...] = total


def owner_sum(n, nh, term):
    key_count, depth = term.shape
    size = key_count // n
    dma = pltpu.SemaphoreType.DMA
    return pl.pallas_call(
        functools.partial(owner_kernel, n, nh),
        out_shape=jax.ShapeDtypeStruct((size, depth), jnp.float32),
        in_specs=[pl.BlockSpec(memory_space=VMEM)],
        out_specs=pl.BlockSpec(memory_space=VMEM),
        scratch_shapes=[
            VMEM((n - 1, size, depth), jnp.bfloat16),
            VMEM((size, depth), jnp.float32),
            VMEM((nh - 1, size, depth), jnp.float32),
            dma((n - 1,)), dma((n - 1,)), dma((nh - 1,)), dma((nh - 1,)),
        ],
        compiler_params=pltpu.CompilerParams(collective_id=2, has_side_effects=True),
        name="owner_sum",
    )(term)


def body(n, nh, latent_queries, latent_keys, index_queries, index_keys, head_weights, visible):
    row_count, gheads, depth = index_queries.shape
    weights_t = head_weights.T
    lat_all, idx_all = gather_keys(n, latent_keys, index_keys)
    logits, split = index_forward(index_queries.reshape(row_count * gheads, depth), weights_t, idx_all)
    me = lax.axis_index("head")
    share = row_count // nh
    mine = lax.dynamic_slice_in_dim(logits, me * share, share, 0)
    for k in range(1, nh):
        leaving = lax.dynamic_slice_in_dim(logits, (me + k) % nh * share, share, 0)
        mine = mine + lax.ppermute(leaving, "head", [(i, (i + k) % nh) for i in range(nh)])
    targets = forward(
        jnp.transpose(latent_queries, (1, 2, 0)), visible.reshape(1, row_count), lat_all
    )
    slope = exchange(nh, mine, targets, visible.reshape(row_count, 1))
    query_grad, weight_grad, term = backward(split, weights_t, idx_all, slope)
    key_grad = owner_sum(n, nh, term)
    return query_grad.reshape(row_count, gheads, depth), weight_grad.T, key_grad


def solution(mesh):
    placed = (
        P("seq", "head", None),
        P("seq", None),
        P("seq", "head", None),
        P("seq", None),
        P("seq", "head"),
        P("seq"),
    )
    return jax.shard_map(
        functools.partial(body, mesh.shape["seq"], mesh.shape["head"]),
        mesh=mesh,
        in_specs=placed,
        out_specs=(P("seq", "head", None), P("seq", "head"), P("seq", None)),
        check_vma=False,
    )
```
